32 devices in a mesh: row: 4 (over z), col: 8 (over y, x, core).
Axes of the slice: x: 2, y: 2, z: 4, core: 2. Of those that a mesh axis runs over, the one named last changes fastest.
Arguments:
- panel_block: bfloat16 [3584, 1024], P(('row', 'col')), may hold values from -1.5 to 1.5
- diag_inverse: bfloat16 [2, 512, 512], replicated
- trailing: bfloat16 [3584, 3584], P('row', 'col'), may hold values from -6 to 6
Outputs:
- factor_panel: bfloat16 [3584, 1024], P(('row', 'col'))
- updated: bfloat16 [3584, 3584], P('row', 'col')
The draws below stay inside these ranges and needn't reach their ends.
All inputs are finite; a program needn't handle non-finite values.
Results may differ from the reference program's by a relative error of at most 0.0054.
Values may be sent and summed in bfloat16 or wider, within the bound.
No kernel may reach another device: no remote copies, remote signals or barrier semaphores. Data moves between devices by JAX's collectives and lax.ppermute only.
A program may use at most 128 MiB of HBM per device.

```python
import math
import jax
import jax.numpy as jnp
from jax import lax

NB = 512
PANELS = 2
CH = 112
RB = 896
M = 3584
N_ROW = 4
N_COL = 8


def draw_diag_inverse(key, part):
    first_key, second_key, third_key = jax.random.split(key, 3)
    spread_size = 0.35 / math.sqrt(NB)
    entries = jnp.clip(jax.random.normal(first_key, (PANELS, NB, NB), jnp.float32), -4.0, 4.0)
    diagonal_values = 0.8 + 0.45 * jax.random.uniform(second_key, (PANELS, NB), jnp.float32)
    top_place = jax.random.randint(third_key, (PANELS, 1), 0, NB)
    positions = lax.broadcasted_iota(jnp.int32, (PANELS, NB), 1)
    diagonal_values = jnp.where(positions == top_place, 1.25, diagonal_values)
    identity = jnp.eye(NB, dtype=jnp.float32)
    matrix = entries * spread_size * (1.0 - identity) + identity * diagonal_values[:, :, None]
    return matrix.astype(jnp.bfloat16)


def steps_of(key, extent, shards, low, top_value):
    loudness, own = 1.0, jax.random.fold_in(key, 6)
    for position, shards_of in shards:
        heights = jnp.exp(jax.random.uniform(jax.random.fold_in(own, position), (shards_of,), jnp.float32, low / len(shards), top_value / len(shards)))
        loudness = loudness * jnp.repeat(heights, extent[position] // shards_of).reshape([-1 if axis == position else 1 for axis in range(len(extent))])
    return loudness


def centred(own_key, dims, deviation, limit, cuts=(), held_as=jnp.bfloat16):
    values = jax.random.normal(own_key, dims, jnp.float32) * deviation
    if len(cuts) > 0:
        values = steps_of(own_key, dims, cuts, -0.22, 0.18) * values
    return jnp.clip(values, min=-limit, max=limit).astype(held_as)


def setup_inputs(seed: int = 0) -> dict:
    key_of = jax.random.split(jax.random.key(seed), 4)
    panel_block = centred(key_of[0], (M, PANELS * NB), 0.25, 1.5, ((0, 32),))
    diag_inverse = draw_diag_inverse(jax.random.fold_in(key_of[3], 71), 0)
    trailing = centred(key_of[2], (M, M), 1.0, 6.0, ((0, 4), (1, 8)))
    return dict(panel_block=panel_block, diag_inverse=diag_inverse, trailing=trailing)


def reference(panel_block, diag_inverse, trailing):
    pieces = []
    for panel in range(PANELS):
        columns = panel_block[:, panel * NB:(panel + 1) * NB]
        pieces.append(jnp.dot(columns, jnp.tril(diag_inverse[panel]).T, preferred_element_type=jnp.float32).astype(jnp.bfloat16))
    factor = jnp.concatenate(pieces, axis=1)
    width = PANELS * NB
    column_factor = factor.reshape(N_ROW, N_COL, CH, width).transpose(1, 0, 2, 3).reshape(N_ROW * N_COL * CH, width)
    right_side = column_factor.astype(jnp.float32)

    def one_block(index):
        start = (index * RB).astype(jnp.int32)
        left_rows = lax.dynamic_slice_in_dim(factor, start, RB, 0).astype(jnp.float32)
        previous = lax.dynamic_slice_in_dim(trailing, start, RB, 0).astype(jnp.float32)
        product = jnp.dot(left_rows, right_side.T, precision=lax.Precision.HIGHEST)
        return (previous - product).astype(jnp.bfloat16)

    blocks = lax.map(one_block, jnp.arange(N_ROW).astype(jnp.int32))
    return factor, blocks.reshape(N_ROW * RB, N_ROW * N_COL * CH)
```

```python
import functools

import jax
import jax.numpy as jnp
from jax import lax
from jax.experimental import pallas as pl
from jax.experimental.pallas import tpu as pltpu
from jax.sharding import PartitionSpec as P

AXES = ("row", "col")
VMEM = pl.BlockSpec(memory_space=pltpu.VMEM)
ANY = pl.BlockSpec(memory_space=pl.ANY)


def column_plan(n):
    if n != 4:
        steps = {f"z{s}": ([(r, r ^ s) for r in range(n)], None) for s in range(1, n)}
        return steps, [(f"z{s}", f"z{s}", s, s) for s in range(1, n)]
    steps = {
        "near": ([(r, r ^ 1) for r in range(n)], None),
        "far": ([(r, r ^ 3) for r in range(n)], None),
        "inward": ([(1, 2), (2, 1)], "near"),
        "outward": ([(1, 0), (2, 3)], "far"),
    }
    blocks = [
        ("near", "near", 1, 1),
        ("far", "outward", 3, 2),
        ("inward", "far", 2, 3),
    ]
    return steps, blocks


def row_plan(n):
    if n != 8:
        steps = {f"c{s}": (s, s, None) for s in range(2, n, 2)}
        return steps, [(name, a, b) for name, (a, b, _) in steps.items()]
    steps = {"first": (2, 4, None), "second": (4, 2, None), "corner": (4, 2, "first")}
    return steps, [("first", 2, 4), ("second", 4, 2), ("corner", 6, 6)]


def factor_of(blocks, inverse_ref):
    panels, width = inverse_ref.shape[0], inverse_ref.shape[1]
    half = width // 2
    pieces = []
    for p in range(panels):
        start = p * width
        for low in (0, half):
            pieces.append(
                lax.dot_general(
                    blocks[:, start : start + low + half],
                    inverse_ref[p, low : low + half, : low + half],
                    (((1,), (1,)), ((), ())),
                    preferred_element_type=jnp.float32,
                ).astype(jnp.bfloat16)
            )
    return jnp.concatenate(pieces, axis=1)


def at(index, rows):
    return pl.ds(pl.multiple_of(index * rows, rows), rows)


def row_index(xors):
    col = lax.axis_index("col")
    return col ^ jnp.where(col % 2 == 0, xors[0], xors[1])


def factor_kernel(row_xors, inverse_ref, *refs):
    n = len(row_xors)
    row_refs, (near_ref,) = refs[:n], refs[n : n + 1]
    factor_ref, rows_ref, near_out, masked_ref, sem = refs[n + 1 :]
    ch = row_refs[0].shape[0]
    panels, width = inverse_ref.shape[0], inverse_ref.shape[1]
    keep = lax.broadcasted_iota(jnp.int32, (width, width), 0) >= lax.broadcasted_iota(
        jnp.int32, (width, width), 1
    )
    for p in range(panels):
        masked_ref[p] = jnp.where(keep, inverse_ref[p].astype(jnp.float32), 0.0).astype(jnp.bfloat16)
    blocks = jnp.concatenate([r[...] for r in row_refs] + [near_ref[...]], axis=0)
    factors = factor_of(blocks, masked_ref)
    for i, xors in enumerate(row_xors):
        rows_ref[at(row_index(xors), ch), :] = factors[i * ch : (i + 1) * ch]
    near_out[...] = factors[n * ch :]
    copy = pltpu.make_async_copy(rows_ref.at[at(row_index((0, 0)), ch), :], factor_ref, sem)
    copy.start()
    copy.wait()


def update(columns, rows_ref, trailing_ref, out_ref, stage_ref, sems, places):
    ch = columns.shape[0] // len(places)
    copies = []
    product = lax.dot_general(
        columns, rows_ref[...], (((1,), (1,)), ((), ())), preferred_element_type=jnp.float32
    )
    for i, place in enumerate(places):
        part = product[i * ch : (i + 1) * ch]
        before = trailing_ref[at(place, ch), :].astype(jnp.float32)
        stage_ref[i] = (before - part).astype(jnp.bfloat16)
        copy = pltpu.make_async_copy(stage_ref.at[i], out_ref.at[at(place, ch), :], sems.at[i])
        copy.start()
        copies.append(copy)
    for copy in copies:
        copy.wait()


def pick(inner, first_ref, second_ref):
    if second_ref is None:
        return first_ref[...]
    return jnp.where(inner, first_ref[...].astype(jnp.float32), second_ref[...].astype(jnp.float32)).astype(
        jnp.bfloat16
    )


def inner_row(n_row):
    row = lax.axis_index("row")
    return (row > 0) & (row < n_row - 1)


def early_kernel(n_row, row_xors, blocks, masked_ref, rows_in, near_ref, trailing_ref, *refs):
    n = len(row_xors)
    late, refs = refs[:n], refs[n:]
    pairs = []
    for a, b, _, _ in blocks[1:]:
        k = 1 if a == b else 2
        pairs.append((refs[0], refs[1] if k == 2 else None))
        refs = refs[k:]
    rows_ref, out_ref, stage_ref, sems = refs
    ch = near_ref.shape[0]
    row, inner = lax.axis_index("row"), inner_row(n_row)
    fresh = [r[...] for r in late] + [pick(inner, *p) for p in pairs]
    factors = factor_of(jnp.concatenate(fresh, axis=0), masked_ref)
    for i, xors in enumerate(row_xors):
        rows_ref[at(row_index(xors), ch), :] = factors[i * ch : (i + 1) * ch]
    own = rows_ref[at(row_index((0, 0)), ch), :]
    columns = jnp.concatenate([own, near_ref[...], factors[n * ch :]], axis=0)
    places = [row] + [row ^ jnp.where(inner, b[2], b[3]) for b in blocks]
    update(columns, rows_ref, trailing_ref, out_ref, stage_ref, sems, places)


def last_kernel(n_row, block, masked_ref, rows_ref, trailing_ref, out_in, *refs):
    k = 1 if block[0] == block[1] else 2
    sent, (out_ref, stage_ref, sems) = refs[:k], refs[k:]
    row, inner = lax.axis_index("row"), inner_row(n_row)
    fresh = pick(inner, sent[0], sent[1] if k == 2 else None)
    columns = factor_of(fresh, masked_ref)
    place = row ^ jnp.where(inner, block[2], block[3])
    update(columns, rows_ref, trailing_ref, out_ref, stage_ref, sems, [place])


def body(n_row, n_col, panel_block, diag_inverse, trailing):
    ch, width = panel_block.shape
    panels, nb = diag_inverse.shape[0], diag_inverse.shape[1]
    own = panel_block

    def send(name, value, pairs):
        with jax.named_scope(name):
            return lax.ppermute(value, AXES, pairs)

    def along_rows(pairs):
        return [(a * n_col + c, b * n_col + c) for a, b in pairs for c in range(n_col)]

    def along_cols(xors):
        return [(r * n_col + c, r * n_col + (c ^ xors[c % 2])) for r in range(n_row) for c in range(n_col)]

    column_steps, column_blocks = column_plan(n_row)
    row_steps, row_blocks = row_plan(n_col)
    got = {}
    for name, (pairs, source) in column_steps.items():
        got[name] = send(name, own if source is None else got[source], along_rows(pairs))
    for name, (even, odd, source) in row_steps.items():
        got[name] = send(name, own if source is None else got[source], along_cols((even, odd)))
    rows = [((0, 0), own), ((1, 1), send("twin", own, along_cols((1, 1))))]
    for name, even, odd in row_blocks:
        rows.append(((even, odd), got[name]))
        rows.append(((odd ^ 1, even ^ 1), send("twin_" + name, got[name], along_cols((1, 1)))))
    early, late = rows[:-2], rows[-2:]

    def cost(factored, updated):
        return pl.CostEstimate(
            flops=2 * ch * width * (nb * factored + n_col * ch * updated),
            bytes_accessed=2 * ch * width * (factored + updated + n_col),
            transcendentals=0,
        )

    def params():
        return pltpu.CompilerParams(vmem_limit_bytes=24 << 20)

    bf16 = lambda *shape: jax.ShapeDtypeStruct(shape, jnp.bfloat16)
    with jax.named_scope("factors"):
        factor, all_rows, near, masked = pl.pallas_call(
            functools.partial(factor_kernel, [x for x, _ in early]),
            out_shape=(bf16(ch, width), bf16(n_col * ch, width), bf16(ch, width), bf16(*diag_inverse.shape)),
            in_specs=[VMEM] * (len(early) + 2),
            out_specs=(ANY, VMEM, VMEM, VMEM),
            scratch_shapes=[pltpu.SemaphoreType.DMA],
            compiler_params=params(),
            cost_estimate=cost(len(early) + 1, 0),
            name="factors",
        )(diag_inverse, *[v for _, v in early], got[column_blocks[0][0]])

    def arrays(block):
        return [got[block[0]]] if block[0] == block[1] else [got[block[0]], got[block[1]]]

    before = trailing.T
    soon, last = column_blocks[:-1], column_blocks[-1]
    k = 1 + len(soon)
    soon_arrays = [a for b in soon[1:] for a in arrays(b)]
    with jax.named_scope("early"):
        all_rows, out = pl.pallas_call(
            functools.partial(early_kernel, n_row, [x for x, _ in late], soon),
            out_shape=(bf16(n_col * ch, width), bf16(n_row * ch, n_col * ch)),
            in_specs=[VMEM] * (4 + len(late) + len(soon_arrays)),
            out_specs=(VMEM, ANY),
            scratch_shapes=[pltpu.VMEM((k, ch, n_col * ch), jnp.bfloat16), pltpu.SemaphoreType.DMA((k,))],
            input_output_aliases={1: 0},
            compiler_params=params(),
            cost_estimate=cost(len(late) + len(soon) - 1, k),
            name="early",
        )(masked, all_rows, near, before, *[v for _, v in late], *soon_arrays)
    with jax.named_scope("last"):
        out = pl.pallas_call(
            functools.partial(last_kernel, n_row, last),
            out_shape=bf16(n_row * ch, n_col * ch),
            in_specs=[VMEM] * 3 + [ANY] + [VMEM] * len(arrays(last)),
            out_specs=ANY,
            scratch_shapes=[pltpu.VMEM((1, ch, n_col * ch), jnp.bfloat16), pltpu.SemaphoreType.DMA((1,))],
            input_output_aliases={3: 0},
            compiler_params=params(),
            cost_estimate=cost(1, 1),
            name="last",
        )(masked, all_rows, before, out, *arrays(last))
    return factor, out.T


def solution(mesh):
    placed = (P(AXES, None), P(), P("row", "col"))
    return jax.shard_map(
        functools.partial(body, mesh.shape["row"], mesh.shape["col"]),
        mesh=mesh,
        in_specs=placed,
        out_specs=(P(AXES, None), P("row", "col")),
        check_vma=False,
    )
```

```python
import functools

import jax
import jax.numpy as jnp
from jax import lax
from jax.experimental import pallas as pl
from jax.experimental.pallas import tpu as pltpu
from jax.sharding import PartitionSpec as P


AXES = ("row", "col")
VMEM = pl.BlockSpec(memory_space=pltpu.VMEM)
HBM = pl.BlockSpec(memory_space=pltpu.HBM)


def column_plan(n):
    if n != 4:
        steps = {f"z{s}": ([(r, r ^ s) for r in range(n)], None) for s in range(1, n)}
        return steps, [(f"z{s}", f"z{s}", s, s) for s in range(1, n)]
    steps = {
        "near": ([(r, r ^ 1) for r in range(n)], None),
        "far": ([(r, r ^ 3) for r in range(n)], None),
        "inward": ([(1, 2), (2, 1)], "near"),
        "outward": ([(1, 0), (2, 3)], "far"),
    }
    blocks = [
        ("near", "near", 1, 1),
        ("far", "outward", 3, 2),
        ("inward", "far", 2, 3),
    ]
    return steps, blocks


def row_plan(n):
    if n != 8:
        steps = {f"c{s}": (s, s, None) for s in range(2, n, 2)}
        return steps, [(name, a, b) for name, (a, b, _) in steps.items()]
    steps = {"first": (2, 4, None), "second": (4, 2, None), "corner": (4, 2, "first")}
    return steps, [("first", 2, 4), ("second", 4, 2), ("corner", 6, 6)]


def factor_of(blocks, inverse_ref):
    panels, width = inverse_ref.shape[0], inverse_ref.shape[1]
    half = width // 2
    pieces = []
    for p in range(panels):
        start = p * width
        for low in (0, half):
            pieces.append(
                lax.dot_general(
                    blocks[:, start : start + low + half],
                    inverse_ref[p, low : low + half, : low + half],
                    (((1,), (1,)), ((), ())),
                    preferred_element_type=jnp.float32,
                ).astype(jnp.bfloat16)
            )
    return jnp.concatenate(pieces, axis=1)


def at(index, rows):
    return pl.ds(pl.multiple_of(index * rows, rows), rows)


def row_index(xors):
    col = lax.axis_index("col")
    return col ^ jnp.where(col % 2 == 0, xors[0], xors[1])


def own_kernel(inverse_ref, own_ref, factor_ref, masked_ref, inverse, own, sems):
    panels, width = inverse.shape[0], inverse.shape[1]
    copies = [
        pltpu.make_async_copy(inverse_ref, inverse, sems.at[0]),
        pltpu.make_async_copy(own_ref, own, sems.at[1]),
    ]
    for copy in copies:
        copy.start()
    keep = lax.broadcasted_iota(jnp.int32, (width, width), 0) >= lax.broadcasted_iota(
        jnp.int32, (width, width), 1
    )
    for copy in copies:
        copy.wait()
    for p in range(panels):
        masked_ref[p] = jnp.where(keep, inverse[p].astype(jnp.float32), 0.0).astype(jnp.bfloat16)
    factor_ref[...] = factor_of(own[...], masked_ref)


def factor_kernel(row_xors, masked_ref, own_ref, *refs):
    n = len(row_xors)
    row_refs, (near_ref,) = refs[:n], refs[n : n + 1]
    factor_ref, rows_ref, near_out, sem = refs[n + 1 :]
    ch = own_ref.shape[0]
    copy = pltpu.make_async_copy(own_ref, factor_ref, sem)
    copy.start()
    blocks = jnp.concatenate([r[...] for r in row_refs] + [near_ref[...]], axis=0)
    factors = factor_of(blocks, masked_ref)
    rows_ref[at(row_index((0, 0)), ch), :] = own_ref[...]
    for i, xors in enumerate(row_xors):
        rows_ref[at(row_index(xors), ch), :] = factors[i * ch : (i + 1) * ch]
    near_out[...] = factors[n * ch :]
    copy.wait()


def update(columns, rows_ref, trailing_ref, out_ref, stage_ref, sems, places):
    ch = columns.shape[0] // len(places)
    copies = []
    product = lax.dot_general(
        columns, rows_ref[...], (((1,), (1,)), ((), ())), preferred_element_type=jnp.float32
    )
    for i, place in enumerate(places):
        part = product[i * ch : (i + 1) * ch]
        before = trailing_ref[at(place, ch), :].astype(jnp.float32)
        stage_ref[i] = (before - part).astype(jnp.bfloat16)
        copy = pltpu.make_async_copy(stage_ref.at[i], out_ref.at[at(place, ch), :], sems.at[i])
        copy.start()
        copies.append(copy)
    for copy in copies:
        copy.wait()


def pick(inner, first_ref, second_ref):
    if second_ref is None:
        return first_ref[...]
    return jnp.where(inner, first_ref[...].astype(jnp.float32), second_ref[...].astype(jnp.float32)).astype(
        jnp.bfloat16
    )


def inner_row(n_row):
    row = lax.axis_index("row")
    return (row > 0) & (row < n_row - 1)


def early_kernel(n_row, row_xors, blocks, masked_ref, rows_in, near_ref, trailing_ref, *refs):
    n = len(row_xors)
    late, refs = refs[:n], refs[n:]
    pairs = []
    for a, b, _, _ in blocks[1:]:
        k = 1 if a == b else 2
        pairs.append((refs[0], refs[1] if k == 2 else None))
        refs = refs[k:]
    rows_ref, out_ref, stage_ref, sems = refs
    ch = near_ref.shape[0]
    row, inner = lax.axis_index("row"), inner_row(n_row)
    fresh = [r[...] for r in late] + [pick(inner, *p) for p in pairs]
    factors = factor_of(jnp.concatenate(fresh, axis=0), masked_ref)
    for i, xors in enumerate(row_xors):
        rows_ref[at(row_index(xors), ch), :] = factors[i * ch : (i + 1) * ch]
    own = rows_ref[at(row_index((0, 0)), ch), :]
    columns = jnp.concatenate([own, near_ref[...], factors[n * ch :]], axis=0)
    places = [row] + [row ^ jnp.where(inner, b[2], b[3]) for b in blocks]
    update(columns, rows_ref, trailing_ref, out_ref, stage_ref, sems, places)


def last_kernel(n_row, block, masked_ref, rows_ref, trailing_ref, out_in, *refs):
    k = 1 if block[0] == block[1] else 2
    sent, (out_ref, stage_ref, sems) = refs[:k], refs[k:]
    row, inner = lax.axis_index("row"), inner_row(n_row)
    fresh = pick(inner, sent[0], sent[1] if k == 2 else None)
    columns = factor_of(fresh, masked_ref)
    place = row ^ jnp.where(inner, block[2], block[3])
    update(columns, rows_ref, trailing_ref, out_ref, stage_ref, sems, [place])


def body(n_row, n_col, panel_block, diag_inverse, trailing):
    ch, width = panel_block.shape
    nb = diag_inverse.shape[1]
    own = panel_block

    def send(value, pairs):
        return lax.ppermute(value, AXES, pairs)

    def along_rows(pairs):
        return [(a * n_col + c, b * n_col + c) for a, b in pairs for c in range(n_col)]

    def along_cols(xors):
        return [(r * n_col + c, r * n_col + (c ^ xors[c % 2])) for r in range(n_row) for c in range(n_col)]

    column_steps, column_blocks = column_plan(n_row)
    row_steps, row_blocks = row_plan(n_col)
    got = {}
    for name, (pairs, source) in column_steps.items():
        got[name] = send(own if source is None else got[source], along_rows(pairs))
    for name, (even, odd, source) in row_steps.items():
        got[name] = send(own if source is None else got[source], along_cols((even, odd)))
    rows = [((1, 1), send(own, along_cols((1, 1))))]
    for name, even, odd in row_blocks:
        rows.append(((even, odd), got[name]))
        rows.append(((odd ^ 1, even ^ 1), send(got[name], along_cols((1, 1)))))
    early, late = rows[:-2], rows[-2:]

    def cost(factored, updated):
        return pl.CostEstimate(
            flops=2 * ch * width * (nb * factored + n_col * ch * updated),
            bytes_accessed=2 * ch * width * (factored + updated + n_col),
            transcendentals=0,
        )

    def params():
        return pltpu.CompilerParams(vmem_limit_bytes=24 << 20)

    bf16 = lambda *shape: jax.ShapeDtypeStruct(shape, jnp.bfloat16)
    own_factor, masked = pl.pallas_call(
        own_kernel,
        out_shape=(bf16(ch, width), bf16(*diag_inverse.shape)),
        in_specs=[HBM, HBM],
        out_specs=(VMEM, VMEM),
        scratch_shapes=[
            pltpu.VMEM(diag_inverse.shape, jnp.bfloat16),
            pltpu.VMEM((ch, width), jnp.bfloat16),
            pltpu.SemaphoreType.DMA((2,)),
        ],
        compiler_params=params(),
        cost_estimate=cost(1, 0),
        name="own",
    )(pltpu.with_memory_space_constraint(diag_inverse, pltpu.HBM), pltpu.with_memory_space_constraint(own, pltpu.HBM))
    factor, all_rows, near = pl.pallas_call(
        functools.partial(factor_kernel, [x for x, _ in early]),
        out_shape=(bf16(ch, width), bf16(n_col * ch, width), bf16(ch, width)),
        in_specs=[VMEM] * (len(early) + 3),
        out_specs=(HBM, VMEM, VMEM),
        scratch_shapes=[pltpu.SemaphoreType.DMA],
        compiler_params=params(),
        cost_estimate=cost(len(early) + 1, 0),
        name="factors",
    )(masked, own_factor, *[v for _, v in early], got[column_blocks[0][0]])

    def arrays(block):
        return [got[block[0]]] if block[0] == block[1] else [got[block[0]], got[block[1]]]

    before = trailing.T
    soon, last = column_blocks[:-1], column_blocks[-1]
    k = 1 + len(soon)
    soon_arrays = [a for b in soon[1:] for a in arrays(b)]
    all_rows, out = pl.pallas_call(
        functools.partial(early_kernel, n_row, [x for x, _ in late], soon),
        out_shape=(bf16(n_col * ch, width), bf16(n_row * ch, n_col * ch)),
        in_specs=[VMEM] * (4 + len(late) + len(soon_arrays)),
        out_specs=(VMEM, HBM),
        scratch_shapes=[pltpu.VMEM((k, ch, n_col * ch), jnp.bfloat16), pltpu.SemaphoreType.DMA((k,))],
        input_output_aliases={1: 0},
        compiler_params=params(),
        cost_estimate=cost(len(late) + len(soon) - 1, k),
        name="early",
    )(masked, all_rows, near, before, *[v for _, v in late], *soon_arrays)
    out = pl.pallas_call(
        functools.partial(last_kernel, n_row, last),
        out_shape=bf16(n_row * ch, n_col * ch),
        in_specs=[VMEM] * 3 + [HBM] + [VMEM] * len(arrays(last)),
        out_specs=HBM,
        scratch_shapes=[pltpu.VMEM((1, ch, n_col * ch), jnp.bfloat16), pltpu.SemaphoreType.DMA((1,))],
        input_output_aliases={3: 0},
        compiler_params=params(),
        cost_estimate=cost(1, 1),
        name="last",
    )(masked, all_rows, before, out, *arrays(last))
    return factor, out.T


def solution(mesh):
    placed = (P(AXES, None), P(), P("row", "col"))

    def step(*args):
        return body(mesh.shape["row"], mesh.shape["col"], *args)

    return jax.shard_map(step, mesh=mesh, in_specs=placed, out_specs=(P(AXES, None), P("row", "col")), check_vma=False)
```
